512 devices in a mesh: sub: 128 (over z_lo, x, y, core), grp: 4 (over z_hi).
Axes of the slice: x: 4, y: 4, z: 16 (z_hi: 4, z_lo: 4; z = z_hi * 4 + z_lo), core: 2. Of those that a mesh axis runs over, the one named last changes fastest.
Arguments:
- load_terms: float32 [128, 4, 512, 384], P('sub', 'grp'), may hold values from -6 to 6
- schur_matrix: float32 [128, 4, 512, 512], P('sub', 'grp'), may hold values from -1 to 4
- local_inverse: float32 [128, 4, 512, 512], P('sub', 'grp'), may hold values from -0.3 to 1
- coarse_modes: float32 [128, 4, 512, 128], P('sub', 'grp'), may hold values from -0.25 to 0.25
- cluster_inverse: float32 [128, 512, 512], P('sub', None, 'grp'), may hold values from -0.5 to 2, as said below
- row_blocks: int32 [128, 4, 4, 96], P('sub', 'grp'), may hold values from 0 to 511, as said below
Outputs:
- solution: float32 [128, 4, 512, 384], P('sub', 'grp')
- residual: float32 [128, 4, 512, 384], P('sub', 'grp')
The draws below stay inside these ranges and needn't reach their ends.
Inputs may be any that keep to these rules, and one draw needn't show every extreme that they name: `row_blocks`: for each subdomain the four blocks hold 384 different rows. `cluster_inverse`: each cluster's matrix is symmetric.
All inputs are finite; a program needn't handle non-finite values.
Results may differ from the reference program's by a relative error of at most 0.00016.
Values sent between devices are 32-bit elements; how exact they have to be, the bound alone decides.
A program may use at most 64 MiB of HBM per device.

```python
import jax
import jax.numpy as jnp
from jax import lax

SCHUR = 512
MODES = 128
SHARED = 96
LOADS = 384
ITERS = 2
ROW_SUBS = 4
CLUSTER = 512
N_SUB = 128
N_GRP = 4


def symmetric_noise(key, count, order, scale):
    noise = jax.random.truncated_normal(key, -4.0, 4.0, (count, order, order), jnp.float32)
    return (noise + jnp.swapaxes(noise, 1, 2)) * (scale / jnp.sqrt(2.0 * order))


def diagonal_matrices(key, count, order, lower, upper, scale):
    first_key, second_key = jax.random.split(key)
    diagonal = jnp.exp(jax.random.uniform(first_key, (count, order), jnp.float32, jnp.log(lower), jnp.log(upper)))
    return symmetric_noise(second_key, count, order, scale) + diagonal[:, :, None] * jnp.eye(order, dtype=jnp.float32)


def draw_schur_matrix(key, part):
    matrices = diagonal_matrices(jax.random.fold_in(key, 11), N_SUB * N_GRP, SCHUR, 1.5, 3.0, 0.6)
    return matrices.reshape(N_SUB, N_GRP, SCHUR, SCHUR)


def draw_local_inverse(key, part):
    matrices = diagonal_matrices(jax.random.fold_in(key, 23), N_SUB * N_GRP, SCHUR, 1.0 / 3.0, 2.0 / 3.0, 0.12)
    return matrices.reshape(N_SUB, N_GRP, SCHUR, SCHUR)


def draw_cluster_inverse(key, part):
    return diagonal_matrices(jax.random.fold_in(key, 37), N_SUB, N_GRP * MODES, 0.5, 1.5, 0.3)


def draw_row_blocks(key, part):
    subkeys = jax.random.split(jax.random.fold_in(key, 41), N_SUB * N_GRP)
    orders = jax.vmap(lambda one_key: jax.random.permutation(one_key, SCHUR))(subkeys)
    return orders[:, :4 * SHARED].reshape(N_SUB, N_GRP, 4, SHARED).astype(jnp.int32)


def block_levels(own_key, extent, pieces, smallest, largest):
    def one(axis_at, shards_of):
        draws = jax.random.uniform(jax.random.fold_in(jax.random.fold_in(own_key, 6), axis_at), (shards_of,), jnp.float32, smallest / len(pieces), largest / len(pieces))
        return jnp.repeat(jnp.exp(draws), extent[axis_at] // shards_of).reshape((-1,) + (1,) * (len(extent) - axis_at - 1))

    factor_of = one(*pieces[0])
    for cut in pieces[1:]:
        factor_of = factor_of * one(*cut)
    return factor_of


def normal_values(rng, shape, scale, reach, shards=(), kind=jnp.bfloat16):
    array = scale * jax.random.normal(rng, shape, jnp.float32)
    if shards:
        array = array * block_levels(rng, shape, shards, -0.22, 0.18)
    return jnp.clip(array, -reach, reach).astype(kind)


def setup_inputs(seed: int = 0) -> dict:
    key_of = jax.random.split(jax.random.key(seed), 7)
    load_terms = normal_values(key_of[0], (N_SUB, N_GRP, SCHUR, LOADS), 1.0, 6.0, ((0, 128), (1, 4)), jnp.float32)
    schur_matrix = draw_schur_matrix(jax.random.fold_in(key_of[6], 71), 0)
    local_inverse = draw_local_inverse(jax.random.fold_in(key_of[6], 71), 0)
    coarse_modes = normal_values(key_of[3], (N_SUB, N_GRP, SCHUR, MODES), SCHUR ** -0.5, 0.25, ((0, 128), (1, 4)), jnp.float32)
    cluster_inverse = draw_cluster_inverse(jax.random.fold_in(key_of[6], 71), 0)
    row_blocks = draw_row_blocks(jax.random.fold_in(key_of[6], 71), 0)
    return {"load_terms": load_terms, "schur_matrix": schur_matrix, "local_inverse": local_inverse, "coarse_modes": coarse_modes, "cluster_inverse": cluster_inverse, "row_blocks": row_blocks}


relax = 0.5
highest = lax.Precision.HIGHEST


def neighbour_present():
    indices = jnp.arange(N_SUB)
    marks = jnp.stack([indices > 0, indices < N_SUB - 1, indices >= ROW_SUBS, indices < N_SUB - ROW_SUBS], axis=1)
    return marks.astype(jnp.float32)


def moved(blocks, offset):
    if offset > 0:
        return jnp.concatenate([jnp.zeros_like(blocks[:offset]), blocks[:-offset]], axis=0)
    return jnp.concatenate([blocks[-offset:], jnp.zeros_like(blocks[:-offset])], axis=0)


def assemble(vectors, flat_rows, present):
    picked = jax.vmap(jax.vmap(lambda column_rows, chosen: column_rows[chosen]))(vectors, flat_rows)
    picked = picked.reshape(N_SUB, N_GRP, 4, SHARED, -1)
    incoming = jnp.stack([moved(picked[:, :, 1], 1), moved(picked[:, :, 0], -1),
                          moved(picked[:, :, 3], ROW_SUBS), moved(picked[:, :, 2], -ROW_SUBS)], axis=2)
    incoming = incoming * present[:, None, :, None, None]
    incoming = incoming.reshape(N_SUB, N_GRP, 4 * SHARED, -1)
    return jax.vmap(jax.vmap(lambda column_rows, chosen, arrivals: column_rows.at[chosen].add(arrivals)))(
        vectors, flat_rows, incoming)


def reference(load_terms, schur_matrix, local_inverse, coarse_modes, cluster_inverse, row_blocks):
    present = neighbour_present()
    flat_rows = row_blocks.reshape(N_SUB, N_GRP, 4 * SHARED).astype(jnp.int32)
    halves = jnp.where(present > 0, 0.5, 1.0)
    marks = jnp.broadcast_to(halves[:, None, :, None], (N_SUB, N_GRP, 4, SHARED)).reshape(N_SUB, N_GRP, -1)
    weight = jax.vmap(jax.vmap(lambda chosen, values: jnp.ones((SCHUR,), jnp.float32).at[chosen].set(values)))(
        flat_rows, marks)[..., None]

    def precondition(current):
        weighted = weight * current
        fine_part = jnp.einsum('sgij,sgjl->sgil', local_inverse, weighted, precision=highest)
        projected = jnp.einsum('sgim,sgil->sgml', coarse_modes, weighted, precision=highest)
        stacked = projected.reshape(N_SUB, CLUSTER, LOADS)
        coarse = jnp.einsum('sij,sjl->sil', cluster_inverse, stacked, precision=highest)
        coarse = coarse.reshape(N_SUB, N_GRP, MODES, LOADS)
        correction = jnp.einsum('sgim,sgml->sgil', coarse_modes, coarse, precision=highest)
        return assemble(weight * (fine_part + correction), flat_rows, present)

    residual = assemble(load_terms, flat_rows, present)
    solution = jnp.zeros_like(load_terms)
    for iteration in range(ITERS):
        solution = solution + relax * precondition(residual)
        product = jnp.einsum('sgij,sgjl->sgil', schur_matrix, solution, precision=highest)
        residual = assemble(load_terms - product, flat_rows, present)
    return solution, residual
```

```python
import functools

import jax
import jax.numpy as jnp
from jax import lax
from jax.experimental import pallas as pl
from jax.experimental.pallas import tpu as pltpu
from jax.sharding import PartitionSpec as P

ITERS = 2
ROW_SUBS = 4
COLS = 128
MESH = pl.DeviceIdType.MESH
F32 = jnp.float32
BF16 = jnp.bfloat16


def split(value):
    high = value.astype(BF16)
    return high, (value - high.astype(F32)).astype(BF16)


def dot(left, right):
    return jnp.dot(left, right, preferred_element_type=F32)


def dot_three(left_high, left_low, right):
    high, low = split(right)
    width = right.shape[1]
    both = dot(left_high, jnp.concatenate([high, low], axis=1))
    return both[:, :width] + both[:, width:] + dot(left_low, high)


def select_rows(chosen, value):
    high, low = split(value)
    width = value.shape[1]
    both = dot(chosen, jnp.concatenate([high, low], axis=1))
    return both[:, :width] + both[:, width:]


def kernel(
    load_ref, schur_ref, solve_ref, modes_ref, cluster_ref, rows_ref,
    x_out, r_out,
    load_v, schur_v, solve_v, modes_v, cluster_v,
    pick, pick_t, schur_h, schur_l, solve_h, solve_l,
    modes_h, modes_l, modes_th, modes_tl, pair_h, pair_l, extra,
    vec, inc, xs, proj, near, own, far_out, far_in, out_x, out_r,
    in_sem, out_sem, a_send, a_recv, n_send, n_recv, f_send, f_recv, e_send, e_recv,
):
    n_sub = lax.axis_size("sub")
    sub = lax.axis_index("sub")
    grp = lax.axis_index("grp")
    rows, loads = load_v.shape
    chunks = loads // COLS
    width = rows_ref.shape[1]
    shared = 4 * width
    rest = rows - shared
    modes = modes_v.shape[1]
    half = COLS // 2
    near_a = grp + 1 - 2 * lax.rem(grp, 2)
    near_b = 3 - grp
    offsets = (-1, 1, -ROW_SUBS, ROW_SUBS)
    targets = [sub + offset for offset in offsets]
    there = [sub > 0, sub < n_sub - 1, sub >= ROW_SUBS, sub < n_sub - ROW_SUBS]

    loads_in = [
        pltpu.make_async_copy(load_ref, load_v, in_sem.at[0]),
        pltpu.make_async_copy(cluster_ref, cluster_v, in_sem.at[1]),
        pltpu.make_async_copy(modes_ref, modes_v, in_sem.at[2]),
        pltpu.make_async_copy(solve_ref, solve_v, in_sem.at[3]),
        pltpu.make_async_copy(schur_ref, schur_v, in_sem.at[4]),
    ]
    for copy in loads_in:
        copy.start()

    barrier = pltpu.get_barrier_semaphore()
    greeted = jnp.int32(2)
    for k in range(4):
        @pl.when(there[k])
        def _():
            pl.semaphore_signal(barrier, 1, device_id=(targets[k], grp), device_id_type=MESH)

        greeted = greeted + there[k].astype(jnp.int32)
    for other in (near_a, near_b):
        pl.semaphore_signal(barrier, 1, device_id=(sub, other), device_id_type=MESH)

    for k in range(4):
        @pl.when(jnp.logical_not(there[k]))
        def _():
            for step in range(2 * ITERS + 1):
                for c in range(chunks):
                    inc[step, c, pl.ds(k * width, width), :] = jnp.zeros((width, COLS), F32)

    def swap(step, c, k):
        rows_at = pl.ds(k * width, width)
        return pltpu.make_async_remote_copy(
            src_ref=vec.at[step, c, rows_at, :],
            dst_ref=inc.at[step, c, pl.ds((k ^ 1) * width, width), :],
            send_sem=a_send.at[step, c, k],
            recv_sem=a_recv.at[step, c, k ^ 1],
            device_id=(targets[k], grp),
            device_id_type=MESH,
        )

    def arrival(step, c, k):
        rows_at = pl.ds(k * width, width)
        return pltpu.make_async_remote_copy(
            src_ref=vec.at[step, c, rows_at, :],
            dst_ref=inc.at[step, c, rows_at, :],
            send_sem=a_send.at[step, c, k],
            recv_sem=a_recv.at[step, c, k],
            device_id=(targets[k], grp),
            device_id_type=MESH,
        )

    def exchange(step, c):
        for k in (2, 3, 0, 1):
            @pl.when(there[k])
            def _():
                swap(step, c, k).start()

    def arrive(step, c):
        for k in (0, 1, 2, 3):
            @pl.when(there[k])
            def _():
                arrival(step, c, k).wait_recv()

    def assembled(step, c):
        return jnp.concatenate(
            [vec[step, c, :shared, :] + inc[step, c], vec[step, c, shared:, :]], axis=0
        )

    def near_copy(it, c, which):
        at = pl.ds(which * half, half)
        return pltpu.make_async_remote_copy(
            src_ref=proj.at[it, c, at, :],
            dst_ref=near.at[it, c, at, :],
            send_sem=n_send.at[it, c, which],
            recv_sem=n_recv.at[it, c, which],
            device_id=(sub, near_b if which else near_a),
            device_id_type=MESH,
        )

    def far_copy(it, c, which):
        at = pl.ds(which * half, half)
        return pltpu.make_async_remote_copy(
            src_ref=far_out.at[it, c, at, :],
            dst_ref=far_in.at[it, c, at, :],
            send_sem=f_send.at[it, c, which],
            recv_sem=f_recv.at[it, c, which],
            device_id=(sub, near_a if which else near_b),
            device_id_type=MESH,
        )

    extra_copy = pltpu.make_async_remote_copy(
        src_ref=cluster_v.at[pl.ds((3 - near_a) * modes, modes), :],
        dst_ref=extra,
        send_sem=e_send,
        recv_sem=e_recv,
        device_id=(sub, near_a),
        device_id_type=MESH,
    )

    eye_i = lax.broadcasted_iota(jnp.int32, (width, width), 0)
    eye_j = lax.broadcasted_iota(jnp.int32, (width, width), 1)
    lane = lax.broadcasted_iota(jnp.int32, (width, rows), 1).astype(F32)
    taken = jnp.zeros((1, rows), F32)
    for k in range(4):
        along = rows_ref[k : k + 1, :].astype(F32)
        column = jnp.sum(jnp.where(eye_i == eye_j, along, 0.0), axis=1, keepdims=True)
        hot = jnp.where(column == lane, 1.0, 0.0)
        taken = taken + jnp.sum(hot, axis=0, keepdims=True)
        pick[k * width : (k + 1) * width, :] = hot.astype(BF16)

    loads_in[0].wait()
    pl.semaphore_wait(barrier, greeted)

    def start(c, carry):
        at = pl.ds(pl.multiple_of(c * COLS, COLS), COLS)
        vec[0, c, :shared, :] = select_rows(pick[:shared, :], load_v[:, at])
        exchange(0, c)
        return carry

    lax.fori_loop(0, chunks, start, 0)
    loads_in[1].wait()
    extra_copy.start()

    free = 1.0 - taken
    order_i = lax.broadcasted_iota(jnp.int32, (rows, rows), 0)
    order_j = lax.broadcasted_iota(jnp.int32, (rows, rows), 1)
    below = jnp.where(order_i < order_j, 1.0, 0.0).astype(BF16)
    rank = dot(jnp.broadcast_to(free, (16, rows)).astype(BF16), below)[:1, :]
    place = lax.broadcasted_iota(jnp.int32, (rest, rows), 0).astype(F32)
    pick[shared:, :] = jnp.where((rank == place) & (free > 0.5), 1.0, 0.0).astype(BF16)
    for c in range(chunks):
        vec[0, c, shared:, :] = select_rows(pick[shared:, :], load_v[:, c * COLS : (c + 1) * COLS])
    for tile in range(rows // 128):
        at = slice(tile * 128, (tile + 1) * 128)
        pick_t[:, at] = jnp.transpose(pick[at, :].astype(F32)).astype(BF16)

    def weights(index):
        total = jnp.ones(index.shape, F32)
        for k in range(4):
            inside = (index >= k * width) & (index < (k + 1) * width)
            total = jnp.where(inside & there[k], 0.5, total)
        return total

    row_weight = weights(lax.broadcasted_iota(jnp.int32, (rows, 1), 0))
    col_weight = weights(lax.broadcasted_iota(jnp.int32, (1, rows), 1))

    loads_in[2].wait()
    basis = row_weight * select_rows(pick[...], modes_v[...])
    modes_h[...], modes_l[...] = split(basis)
    modes_th[...], modes_tl[...] = split(jnp.transpose(basis))

    def reorder(matrix, high_ref, low_ref, scale):
        tile = 128
        for part, into in zip(split(matrix[...]), (high_ref, low_ref)):
            for i in range(rows // tile):
                at = slice(i * tile, (i + 1) * tile)
                moved = dot(pick[at, :], part).astype(BF16)
                moved = dot(moved, pick_t[...])
                if scale is not None:
                    moved = moved * (scale * row_weight[at, :] * col_weight)
                into[at, :] = moved.astype(BF16)

    loads_in[3].wait()
    reorder(solve_v, solve_h, solve_l, 0.5)

    def project(it, c):
        step = 2 * it
        arrive(step, c)
        current = assembled(step, c)
        terms = dot_three(modes_th[...], modes_tl[...], current)
        proj[it, c] = jnp.transpose(terms)
        near_copy(it, c, 0).start()
        near_copy(it, c, 1).start()

    def fine(it, c):
        step = 2 * it
        vec[step + 1, c] = dot_three(solve_h[...], solve_l[...], assembled(step, c))

    def pairs():
        def block(k):
            return 0.5 * cluster_v[pl.ds(pl.multiple_of(k * modes, modes), modes), :]

        to_a, to_b, same = block(near_a), block(near_b), block(grp)
        extra_copy.wait_recv()
        cross = 0.5 * extra[...]
        first = jnp.concatenate(
            [
                jnp.concatenate([jnp.transpose(to_b), same], axis=1),
                jnp.concatenate([jnp.transpose(cross), to_a], axis=1),
            ],
            axis=0,
        )
        second = jnp.concatenate(
            [
                jnp.concatenate([jnp.transpose(to_a), same], axis=1),
                jnp.concatenate([cross, to_b], axis=1),
            ],
            axis=0,
        )
        pair_h[0], pair_l[0] = split(first)
        pair_h[1], pair_l[1] = split(second)

    def combine(it, c):
        for which in range(2):
            at = slice(which * half, (which + 1) * half)
            near_copy(it, c, which).wait_recv()
            known = jnp.concatenate([proj[it, c, at, :], near[it, c, at, :]], axis=1)
            high, low = split(known)
            mixed = (
                dot(high, pair_h[which]) + dot(low, pair_h[which]) + dot(high, pair_l[which])
            )
            far_out[it, c, at, :] = mixed[:, :modes]
            far_copy(it, c, which).start()
            own[c, at, :] = mixed[:, modes:]

    def correct(it, c):
        for which in range(2):
            far_copy(it, c, which).wait_recv()
        coarse = jnp.transpose(own[c] + far_in[it, c])
        step = 2 * it + 1
        vec[step, c] = vec[step, c] + dot_three(modes_h[...], modes_l[...], coarse)
        exchange(step, c)

    def advance(it, c):
        step = 2 * it + 1
        arrive(step, c)
        value = assembled(step, c)
        if it > 0:
            value = value + xs[c]
        xs[c] = value
        vec[step + 1, c] = vec[0, c] - dot_three(schur_h[...], schur_l[...], value)
        exchange(step + 1, c)

    def every(stage, *args):
        def body(c, carry):
            stage(*args, c)
            return carry

        lax.fori_loop(0, chunks, body, 0)

    for it in range(ITERS):
        every(project, it)
        if it == 0:
            pairs()
        every(fine, it)
        every(combine, it)
        if it == 0:
            loads_in[4].wait()
            reorder(schur_v, schur_h, schur_l, None)
        every(correct, it)
        every(advance, it)

    for c in range(chunks):
        at = pl.ds(c * COLS, COLS)
        out_x[:, c * COLS : (c + 1) * COLS] = select_rows(pick_t[...], xs[c])
    write_x = pltpu.make_async_copy(out_x, x_out, out_sem.at[0])
    write_x.start()
    last = 2 * ITERS
    for c in range(chunks):
        arrive(last, c)
        out_r[:, c * COLS : (c + 1) * COLS] = select_rows(pick_t[...], assembled(last, c))
    write_r = pltpu.make_async_copy(out_r, r_out, out_sem.at[1])
    write_r.start()

    extra_copy.wait_send()

    def drain(c, carry):
        for step in range(2 * ITERS + 1):
            for k in range(4):
                @pl.when(there[k])
                def _():
                    swap(step, c, k).wait_send()
        for it in range(ITERS):
            for which in range(2):
                near_copy(it, c, which).wait_send()
                far_copy(it, c, which).wait_send()
        return carry

    lax.fori_loop(0, chunks, drain, 0)
    write_x.wait()
    write_r.wait()


def local(load_terms, schur_matrix, local_inverse, coarse_modes, cluster_inverse, row_blocks):
    rows, loads = load_terms.shape[2:]
    modes = coarse_modes.shape[3]
    width = row_blocks.shape[3]
    chunks = loads // COLS
    steps = 2 * ITERS + 1
    half = COLS // 2
    any_spec = pl.BlockSpec(memory_space=pl.ANY)
    vmem_spec = pl.BlockSpec(memory_space=pltpu.VMEM)
    dma = pltpu.SemaphoreType.DMA
    out = jax.ShapeDtypeStruct((rows, loads), F32)
    solution, residual = pl.pallas_call(
        kernel,
        out_shape=(out, out),
        in_specs=[any_spec] * 5 + [vmem_spec],
        out_specs=(any_spec, any_spec),
        scratch_shapes=[
            pltpu.VMEM((rows, loads), F32),
            pltpu.VMEM((rows, rows), F32),
            pltpu.VMEM((rows, rows), F32),
            pltpu.VMEM((rows, modes), F32),
            pltpu.VMEM(cluster_inverse.shape[1:], F32),
            pltpu.VMEM((rows, rows), BF16),
            pltpu.VMEM((rows, rows), BF16),
            pltpu.VMEM((rows, rows), BF16),
            pltpu.VMEM((rows, rows), BF16),
            pltpu.VMEM((rows, rows), BF16),
            pltpu.VMEM((rows, rows), BF16),
            pltpu.VMEM((rows, modes), BF16),
            pltpu.VMEM((rows, modes), BF16),
            pltpu.VMEM((modes, rows), BF16),
            pltpu.VMEM((modes, rows), BF16),
            pltpu.VMEM((2, 2 * modes, 2 * modes), BF16),
            pltpu.VMEM((2, 2 * modes, 2 * modes), BF16),
            pltpu.VMEM((modes, modes), F32),
            pltpu.VMEM((steps, chunks, rows, COLS), F32),
            pltpu.VMEM((steps, chunks, 4 * width, COLS), F32),
            pltpu.VMEM((chunks, rows, COLS), F32),
            pltpu.VMEM((ITERS, chunks, COLS, modes), F32),
            pltpu.VMEM((ITERS, chunks, COLS, modes), F32),
            pltpu.VMEM((chunks, COLS, modes), F32),
            pltpu.VMEM((ITERS, chunks, COLS, modes), F32),
            pltpu.VMEM((ITERS, chunks, COLS, modes), F32),
            pltpu.VMEM((rows, loads), F32),
            pltpu.VMEM((rows, loads), F32),
            dma((5,)),
            dma((2,)),
            dma((steps, chunks, 4)),
            dma((steps, chunks, 4)),
            dma((ITERS, chunks, 2)),
            dma((ITERS, chunks, 2)),
            dma((ITERS, chunks, 2)),
            dma((ITERS, chunks, 2)),
            dma,
            dma,
        ],
        compiler_params=pltpu.CompilerParams(
            collective_id=0, has_side_effects=True, vmem_limit_bytes=60 * 1024 * 1024
        ),
    )(
        load_terms[0, 0], schur_matrix[0, 0], local_inverse[0, 0], coarse_modes[0, 0],
        cluster_inverse[0], row_blocks[0, 0],
    )
    return solution[None, None], residual[None, None]


def solution(mesh):
    return jax.shard_map(
        local,
        mesh=mesh,
        in_specs=(
            P("sub", "grp", None, None),
            P("sub", "grp", None, None),
            P("sub", "grp", None, None),
            P("sub", "grp", None, None),
            P("sub", None, "grp"),
            P("sub", "grp", None, None),
        ),
        out_specs=(P("sub", "grp", None, None), P("sub", "grp", None, None)),
        check_vma=False,
    )
```

```python
import functools

import jax
import jax.numpy as jnp
from jax import lax
from jax.experimental import pallas as pl
from jax.experimental.pallas import tpu as pltpu
from jax.sharding import PartitionSpec as P

ITERS = 2
ROW_SUBS = 4
COLS = 128
HALF = 64
MESH = pl.DeviceIdType.MESH
F32 = jnp.float32
BF16 = jnp.bfloat16


def split(value):
    high = value.astype(BF16)
    return high, (value - high.astype(F32)).astype(BF16)


def dot(left, right):
    return jnp.dot(left, right, preferred_element_type=F32)


def select_rows(chosen, value):
    high, low = split(value)
    width = value.shape[1]
    both = dot(chosen, jnp.concatenate([high, low], axis=1))
    return both[:, :width] + both[:, width:]


def left_lanes(shape):
    return lax.broadcasted_iota(jnp.int32, shape, 1) < HALF


def turn(value):
    return pltpu.roll(value, HALF, 1)


def parts(packed):
    left = left_lanes(packed.shape)
    high = packed.astype(BF16).astype(F32)
    low = packed - high
    top = jnp.where(left, high, turn(low))
    bottom = jnp.where(left, turn(high), low)
    return jnp.concatenate([top, bottom], axis=0).astype(BF16)


def fold(product):
    middle = product.shape[0] // 2
    top, bottom = product[:middle], product[middle:]
    left = left_lanes(top.shape)
    return jnp.where(left, top + turn(top), bottom + turn(bottom))


def twice(value):
    return jnp.concatenate([value, value], axis=0)


def kernel(
    load_ref, schur_ref, solve_ref, modes_ref, cluster_ref, rows_ref,
    both_out,
    load_v, schur_v, solve_v, modes_v, cluster_v,
    pick, pick_t, schur_hl, solve_hl, modes_hl, modes_thl, pair_h, pair_l, extra,
    vec, inc, xs, rhs, proj, near, own, far_out, far_in, out_x, out_r,
    in_sem, out_sem, a_send, a_recv, n_send, n_recv, f_send, f_recv, e_send, e_recv,
):
    n_sub = lax.axis_size("sub")
    sub = lax.axis_index("sub")
    grp = lax.axis_index("grp")
    rows, loads = load_v.shape
    blocks = loads // COLS
    chunks = 2 * blocks
    width = rows_ref.shape[1]
    piece = width // 2
    middle = rows // 2
    shared = 4 * piece
    modes = modes_v.shape[1]
    share = HALF // 2
    steps = 2 * ITERS + 1
    near_a = grp + 1 - 2 * lax.rem(grp, 2)
    near_b = 3 - grp
    offsets = (-1, 1, -ROW_SUBS, ROW_SUBS)
    targets = [sub + offset for offset in offsets]
    there = [sub > 0, sub < n_sub - 1, sub >= ROW_SUBS, sub < n_sub - ROW_SUBS]

    loads_in = [
        pltpu.make_async_copy(load_ref, load_v, in_sem.at[0]),
        pltpu.make_async_copy(cluster_ref, cluster_v, in_sem.at[1]),
        pltpu.make_async_copy(modes_ref, modes_v, in_sem.at[2]),
        pltpu.make_async_copy(solve_ref, solve_v, in_sem.at[3]),
        pltpu.make_async_copy(schur_ref, schur_v, in_sem.at[4]),
    ]
    for copy in loads_in:
        copy.start()

    barrier = pltpu.get_barrier_semaphore()
    greeted = jnp.int32(2)
    for k in range(4):
        @pl.when(there[k])
        def _():
            pl.semaphore_signal(barrier, 1, device_id=(targets[k], grp), device_id_type=MESH)

        greeted = greeted + there[k].astype(jnp.int32)
    for other in (near_a, near_b):
        pl.semaphore_signal(barrier, 1, device_id=(sub, other), device_id_type=MESH)

    for k in range(4):
        @pl.when(jnp.logical_not(there[k]))
        def _():
            def clear(c, carry):
                for step in range(steps):
                    inc[step, c, pl.ds(k * piece, piece), :] = jnp.zeros((piece, COLS), F32)
                return carry

            lax.fori_loop(0, chunks, clear, 0)

    def swap(step, c, k):
        return pltpu.make_async_remote_copy(
            src_ref=vec.at[step, c, pl.ds(k * piece, piece), :],
            dst_ref=inc.at[step, c, pl.ds((k ^ 1) * piece, piece), :],
            send_sem=a_send.at[c, k],
            recv_sem=a_recv.at[step, c, k ^ 1],
            device_id=(targets[k], grp),
            device_id_type=MESH,
        )

    def arrival(step, c, k):
        rows_at = pl.ds(k * piece, piece)
        return pltpu.make_async_remote_copy(
            src_ref=vec.at[step, c, rows_at, :],
            dst_ref=inc.at[step, c, rows_at, :],
            send_sem=a_send.at[c, k],
            recv_sem=a_recv.at[step, c, k],
            device_id=(targets[k], grp),
            device_id_type=MESH,
        )

    def exchange(step, c):
        for k in (2, 3, 0, 1):
            @pl.when(there[k])
            def _():
                if step > 0:
                    swap(step - 1, c, k).wait_send()
                swap(step, c, k).start()

    def arrive(step, c):
        for k in (0, 1, 2, 3):
            @pl.when(there[k])
            def _():
                arrival(step, c, k).wait_recv()

    def assembled(step, c):
        return jnp.concatenate(
            [vec[step, c, :shared, :] + inc[step, c], vec[step, c, shared:, :]], axis=0
        )

    def near_copy(it, c, which):
        at = pl.ds(which * share, share)
        return pltpu.make_async_remote_copy(
            src_ref=proj.at[it, c, at, :],
            dst_ref=near.at[it, c, at, :],
            send_sem=n_send.at[c, which],
            recv_sem=n_recv.at[it, c, which],
            device_id=(sub, near_b if which else near_a),
            device_id_type=MESH,
        )

    def far_copy(it, c, which):
        at = pl.ds(which * share, share)
        return pltpu.make_async_remote_copy(
            src_ref=far_out.at[it, c, at, :],
            dst_ref=far_in.at[it, c, at, :],
            send_sem=f_send.at[c, which],
            recv_sem=f_recv.at[it, c, which],
            device_id=(sub, near_a if which else near_b),
            device_id_type=MESH,
        )

    extra_copy = pltpu.make_async_remote_copy(
        src_ref=cluster_v.at[pl.ds((3 - near_a) * modes, modes), :],
        dst_ref=extra,
        send_sem=e_send,
        recv_sem=e_recv,
        device_id=(sub, near_a),
        device_id_type=MESH,
    )

    eye_i = lax.broadcasted_iota(jnp.int32, (width, width), 0)
    eye_j = lax.broadcasted_iota(jnp.int32, (width, width), 1)
    lane = lax.broadcasted_iota(jnp.int32, (width, rows), 1).astype(F32)
    taken = jnp.zeros((1, rows), F32)
    for k in range(4):
        along = rows_ref[k : k + 1, :].astype(F32)
        column = jnp.sum(jnp.where(eye_i == eye_j, along, 0.0), axis=1, keepdims=True)
        hot = jnp.where(column == lane, 1.0, 0.0)
        taken = taken + jnp.sum(hot, axis=0, keepdims=True)
        hot = hot.astype(BF16)
        pick[k * piece : (k + 1) * piece, :] = hot[:piece]
        pick[middle + k * piece : middle + (k + 1) * piece, :] = hot[piece:]

    loads_in[0].wait()
    pl.semaphore_wait(barrier, greeted)

    def pack_pair(top, bottom, step, j, at):
        left = left_lanes(top.shape)
        vec[step, 2 * j, at, :] = jnp.where(left, top, turn(bottom))
        vec[step, 2 * j + 1, at, :] = jnp.where(left, turn(top), bottom)

    def start(j, carry):
        at = pl.ds(pl.multiple_of(j * COLS, COLS), COLS)
        chosen = jnp.concatenate([pick[:shared, :], pick[middle : middle + shared, :]], axis=0)
        moved = select_rows(chosen, load_v[:, at])
        pack_pair(moved[:shared], moved[shared:], 0, j, pl.ds(0, shared))
        exchange(0, 2 * j)
        exchange(0, 2 * j + 1)
        return carry

    lax.fori_loop(0, blocks, start, 0)
    loads_in[1].wait()
    extra_copy.start()

    spare = middle - shared
    free = 1.0 - taken
    order_i = lax.broadcasted_iota(jnp.int32, (rows, rows), 0)
    order_j = lax.broadcasted_iota(jnp.int32, (rows, rows), 1)
    below = jnp.where(order_i < order_j, 1.0, 0.0).astype(BF16)
    rank = dot(jnp.broadcast_to(free, (16, rows)).astype(BF16), below)[:1, :]
    place = lax.broadcasted_iota(jnp.int32, (2 * spare, rows), 0).astype(F32)
    others = jnp.where((rank == place) & (free > 0.5), 1.0, 0.0).astype(BF16)
    pick[shared:middle, :] = others[:spare]
    pick[middle + shared :, :] = others[spare:]
    for j in range(blocks):
        moved = select_rows(others, load_v[:, j * COLS : (j + 1) * COLS])
        pack_pair(moved[:spare], moved[spare:], 0, j, pl.ds(shared, spare))

    def weights(index):
        within = lax.rem(index, middle)
        total = jnp.ones(index.shape, F32)
        for k in range(4):
            inside = (within >= k * piece) & (within < (k + 1) * piece)
            total = jnp.where(inside & there[k], 0.5, total)
        return total

    row_weight = weights(lax.broadcasted_iota(jnp.int32, (rows, 1), 0))
    col_weight = weights(lax.broadcasted_iota(jnp.int32, (1, rows), 1))

    loads_in[2].wait()
    basis = row_weight * select_rows(pick[...], modes_v[...])
    high, low = split(basis)
    modes_hl[:, :modes] = high
    modes_hl[:, modes:] = low
    high, low = split(jnp.transpose(basis))
    modes_thl[:, :rows] = high
    modes_thl[:, rows:] = low

    def reorder(matrix, into, scale):
        tile = 128
        for p, part in enumerate(split(matrix[...])):
            for i in range(rows // tile):
                at = slice(i * tile, (i + 1) * tile)
                moved = dot(pick[at, :], part).astype(BF16)
                moved = dot(moved, pick_t[...])
                if scale is not None:
                    moved = moved * (scale * row_weight[at, :] * col_weight)
                into[at, p * rows : (p + 1) * rows] = moved.astype(BF16)

    def project(it, c):
        step = 2 * it
        arrive(step, c)
        sides = parts(assembled(step, c))
        rhs[c] = sides
        terms = jnp.transpose(dot(modes_thl[...], twice(sides)))
        if it > 0:
            for which in range(2):
                near_copy(it - 1, c, which).wait_send()
        proj[it, c] = terms[:HALF] + terms[HALF:]
        near_copy(it, c, 0).start()
        near_copy(it, c, 1).start()

    def fine(it, j):
        step = 2 * it + 1
        sides = jnp.concatenate([rhs[2 * j], rhs[2 * j + 1]], axis=1)
        both = dot(solve_hl[...], twice(sides))
        vec[step, 2 * j] = fold(both[:, :COLS])
        vec[step, 2 * j + 1] = fold(both[:, COLS:])

    def pairs():
        def block(k):
            return 0.5 * cluster_v[pl.ds(pl.multiple_of(k * modes, modes), modes), :]

        to_a, to_b, same = block(near_a), block(near_b), block(grp)
        extra_copy.wait_recv()
        cross = 0.5 * extra[...]
        first = jnp.concatenate(
            [
                jnp.concatenate([jnp.transpose(to_b), same], axis=1),
                jnp.concatenate([jnp.transpose(cross), to_a], axis=1),
            ],
            axis=0,
        )
        second = jnp.concatenate(
            [
                jnp.concatenate([jnp.transpose(to_a), same], axis=1),
                jnp.concatenate([cross, to_b], axis=1),
            ],
            axis=0,
        )
        pair_h[0], pair_l[0] = split(first)
        pair_h[1], pair_l[1] = split(second)

    def combine(it, c):
        for which in range(2):
            at = slice(which * share, (which + 1) * share)
            near_copy(it, c, which).wait_recv()
            known = jnp.concatenate([proj[it, c, at, :], near[it, c, at, :]], axis=1)
            high, low = split(known)
            mixed = dot(jnp.concatenate([high, low], axis=0), pair_h[which])
            mixed = mixed[:share] + mixed[share:] + dot(high, pair_l[which])
            if it > 0:
                far_copy(it - 1, c, which).wait_send()
            far_out[it, c, at, :] = mixed[:, :modes]
            far_copy(it, c, which).start()
            own[c, at, :] = mixed[:, modes:]

    def correct(it, c):
        for which in range(2):
            far_copy(it, c, which).wait_recv()
        coarse = own[c] + far_in[it, c]
        high = coarse.astype(BF16).astype(F32)
        sides = jnp.transpose(jnp.concatenate([high, coarse - high], axis=0)).astype(BF16)
        step = 2 * it + 1
        vec[step, c] = vec[step, c] + fold(dot(modes_hl[...], twice(sides)))
        exchange(step, c)

    def advance(it, c):
        step = 2 * it + 1
        arrive(step, c)
        value = assembled(step, c)
        if it > 0:
            value = value + xs[c]
        xs[c] = value
        vec[step + 1, c] = vec[0, c] - fold(dot(schur_hl[...], twice(parts(value))))
        exchange(step + 1, c)

    def every(stage, it, count):
        def body(c, carry):
            stage(it, c)
            return carry

        lax.fori_loop(0, count, body, 0)

    for it in range(ITERS):
        every(project, it, chunks)
        if it == 0:
            for tile in range(rows // 128):
                at = slice(tile * 128, (tile + 1) * 128)
                pick_t[:, at] = jnp.transpose(pick[at, :].astype(F32)).astype(BF16)
            pairs()
            loads_in[3].wait()
            reorder(solve_v, solve_hl, 0.5)
        if it > 0:
            every(fine, it, blocks)
        every(combine, it, chunks)
        if it == 0:
            every(fine, it, blocks)
            loads_in[4].wait()
            reorder(schur_v, schur_hl, None)
        every(correct, it, chunks)
        every(advance, it, chunks)

    def unpacked(first, second):
        left = left_lanes(first.shape)
        return jnp.concatenate(
            [jnp.where(left, first, turn(second)), jnp.where(left, turn(first), second)], axis=0
        )

    for j in range(blocks):
        at = slice(j * COLS, (j + 1) * COLS)
        out_x[:, at] = 0.5 * select_rows(pick_t[...], unpacked(xs[2 * j], xs[2 * j + 1]))
    write_x = pltpu.make_async_copy(out_x, both_out.at[0], out_sem.at[0])
    write_x.start()
    last = 2 * ITERS
    writes = []
    for j in range(blocks):
        at = slice(j * COLS, (j + 1) * COLS)
        arrive(last, 2 * j)
        arrive(last, 2 * j + 1)
        value = unpacked(assembled(last, 2 * j), assembled(last, 2 * j + 1))
        out_r[j] = 0.5 * select_rows(pick_t[...], value)
        write = pltpu.make_async_copy(
            out_r.at[j], both_out.at[1, :, pl.ds(j * COLS, COLS)], out_sem.at[1 + j]
        )
        write.start()
        writes.append(write)

    extra_copy.wait_send()

    def drain(c, carry):
        for k in range(4):
            @pl.when(there[k])
            def _():
                swap(last, c, k).wait_send()
        for which in range(2):
            near_copy(ITERS - 1, c, which).wait_send()
            far_copy(ITERS - 1, c, which).wait_send()
        return carry

    lax.fori_loop(0, chunks, drain, 0)
    write_x.wait()
    for write in writes:
        write.wait()


def local(load_terms, schur_matrix, local_inverse, coarse_modes, cluster_inverse, row_blocks):
    rows, loads = load_terms.shape[2:]
    modes = coarse_modes.shape[3]
    width = row_blocks.shape[3]
    blocks = loads // COLS
    chunks = 2 * blocks
    steps = 2 * ITERS + 1
    any_spec = pl.BlockSpec(memory_space=pl.ANY)
    vmem_spec = pl.BlockSpec(memory_space=pltpu.VMEM)
    dma = pltpu.SemaphoreType.DMA
    halves = pl.pallas_call(
        kernel,
        out_shape=jax.ShapeDtypeStruct((2, rows, loads), F32),
        in_specs=[any_spec] * 5 + [vmem_spec],
        out_specs=any_spec,
        scratch_shapes=[
            pltpu.VMEM((rows, loads), F32),
            pltpu.VMEM((rows, rows), F32),
            pltpu.VMEM((rows, rows), F32),
            pltpu.VMEM((rows, modes), F32),
            pltpu.VMEM(cluster_inverse.shape[1:], F32),
            pltpu.VMEM((rows, rows), BF16),
            pltpu.VMEM((rows, rows), BF16),
            pltpu.VMEM((rows, 2 * rows), BF16),
            pltpu.VMEM((rows, 2 * rows), BF16),
            pltpu.VMEM((rows, 2 * modes), BF16),
            pltpu.VMEM((modes, 2 * rows), BF16),
            pltpu.VMEM((2, 2 * modes, 2 * modes), BF16),
            pltpu.VMEM((2, 2 * modes, 2 * modes), BF16),
            pltpu.VMEM((modes, modes), F32),
            pltpu.VMEM((steps, chunks, rows // 2, COLS), F32),
            pltpu.VMEM((steps, chunks, 2 * width, COLS), F32),
            pltpu.VMEM((chunks, rows // 2, COLS), F32),
            pltpu.VMEM((chunks, rows, COLS), BF16),
            pltpu.VMEM((ITERS, chunks, HALF, modes), F32),
            pltpu.VMEM((ITERS, chunks, HALF, modes), F32),
            pltpu.VMEM((chunks, HALF, modes), F32),
            pltpu.VMEM((ITERS, chunks, HALF, modes), F32),
            pltpu.VMEM((ITERS, chunks, HALF, modes), F32),
            pltpu.VMEM((rows, loads), F32),
            pltpu.VMEM((blocks, rows, COLS), F32),
            dma((5,)),
            dma((1 + blocks,)),
            dma((chunks, 4)),
            dma((steps, chunks, 4)),
            dma((chunks, 2)),
            dma((ITERS, chunks, 2)),
            dma((chunks, 2)),
            dma((ITERS, chunks, 2)),
            dma,
            dma,
        ],
        compiler_params=pltpu.CompilerParams(
            collective_id=0, has_side_effects=True, vmem_limit_bytes=60 * 1024 * 1024
        ),
    )(
        load_terms[0, 0], schur_matrix[0, 0], local_inverse[0, 0], coarse_modes[0, 0],
        cluster_inverse[0], row_blocks[0, 0],
    )
    return 2.0 * halves[0][None, None], 2.0 * halves[1][None, None]


def solution(mesh):
    return jax.shard_map(
        local,
        mesh=mesh,
        in_specs=(
            P("sub", "grp", None, None),
            P("sub", "grp", None, None),
            P("sub", "grp", None, None),
            P("sub", "grp", None, None),
            P("sub", None, "grp"),
            P("sub", "grp", None, None),
        ),
        out_specs=(P("sub", "grp", None, None), P("sub", "grp", None, None)),
        check_vma=False,
    )
```

```python
import functools

import jax
import jax.numpy as jnp
from jax import lax
from jax.experimental import pallas as pl
from jax.experimental.pallas import tpu as pltpu
from jax.sharding import PartitionSpec as P

ITERS = 2
ROW_SUBS = 4
COLS = 128
HALF = 64
MESH = pl.DeviceIdType.MESH
F32 = jnp.float32
BF16 = jnp.bfloat16


def split(value):
    high = value.astype(BF16)
    return high, (value - high.astype(F32)).astype(BF16)


def dot(left, right):
    return jnp.dot(left, right, preferred_element_type=F32)


def select_rows(chosen, value):
    high, low = split(value)
    width = value.shape[1]
    both = dot(chosen, jnp.concatenate([high, low], axis=1))
    return both[:, :width] + both[:, width:]


def left_lanes(shape):
    return lax.broadcasted_iota(jnp.int32, shape, 1) < HALF


def turn(value):
    return pltpu.roll(value, HALF, 1)


def parts(packed):
    left = left_lanes(packed.shape)
    high = packed.astype(BF16).astype(F32)
    low = packed - high
    top = jnp.where(left, high, turn(low))
    bottom = jnp.where(left, turn(high), low)
    return jnp.concatenate([top, bottom], axis=0).astype(BF16)


def fold(product):
    middle = product.shape[0] // 2
    top, bottom = product[:middle], product[middle:]
    left = left_lanes(top.shape)
    return jnp.where(left, top + turn(top), bottom + turn(bottom))


def twice(value):
    return jnp.concatenate([value, value], axis=0)


def kernel(
    load_ref, schur_ref, solve_ref, modes_ref, cluster_ref, rows_ref,
    both_out,
    load_v, schur_v, solve_v, modes_v, cluster_v,
    pick, pick_t, schur_hl, solve_hl, modes_hl, modes_thl, pair_h, pair_l, extra, extra_out,
    vec, inc, xs, rhs, proj, near, own, far_out, far_in, out_x, out_r,
    in_sem, out_sem, a_send, a_recv, n_send, n_recv, f_send, f_recv, e_send, e_recv,
):
    n_sub = lax.axis_size("sub")
    sub = lax.axis_index("sub")
    grp = lax.axis_index("grp")
    rows, loads = load_v.shape
    blocks = loads // COLS
    chunks = 2 * blocks
    width = rows_ref.shape[1]
    piece = width // 2
    middle = rows // 2
    shared = 4 * piece
    modes = modes_v.shape[1]
    share = HALF // 2
    steps = 2 * ITERS + 1
    near_a = grp + 1 - 2 * lax.rem(grp, 2)
    near_b = 3 - grp
    offsets = (-1, 1, -ROW_SUBS, ROW_SUBS)
    targets = [sub + offset for offset in offsets]
    there = [sub > 0, sub < n_sub - 1, sub >= ROW_SUBS, sub < n_sub - ROW_SUBS]

    loads_in = [
        pltpu.make_async_copy(load_ref, load_v, in_sem.at[0]),
        pltpu.make_async_copy(cluster_ref, cluster_v, in_sem.at[1]),
        pltpu.make_async_copy(modes_ref, modes_v, in_sem.at[2]),
        pltpu.make_async_copy(solve_ref, solve_v, in_sem.at[3]),
        pltpu.make_async_copy(schur_ref, schur_v, in_sem.at[4]),
    ]
    for copy in loads_in:
        copy.start()

    barrier = pltpu.get_barrier_semaphore()
    greeted = jnp.int32(2)
    for k in range(4):
        @pl.when(there[k])
        def _():
            pl.semaphore_signal(barrier, 1, device_id=(targets[k], grp), device_id_type=MESH)

        greeted = greeted + there[k].astype(jnp.int32)
    for other in (near_a, near_b):
        pl.semaphore_signal(barrier, 1, device_id=(sub, other), device_id_type=MESH)

    for k in range(4):
        @pl.when(jnp.logical_not(there[k]))
        def _():
            def clear(c, carry):
                for step in range(steps):
                    inc[step, c, pl.ds(k * piece, piece), :] = jnp.zeros((piece, COLS), F32)
                return carry

            lax.fori_loop(0, chunks, clear, 0)

    def swap(step, c, k):
        return pltpu.make_async_remote_copy(
            src_ref=vec.at[step, c, pl.ds(k * piece, piece), :],
            dst_ref=inc.at[step, c, pl.ds((k ^ 1) * piece, piece), :],
            send_sem=a_send.at[c, k],
            recv_sem=a_recv.at[step, c, k ^ 1],
            device_id=(targets[k], grp),
            device_id_type=MESH,
        )

    def arrival(step, c, k):
        rows_at = pl.ds(k * piece, piece)
        return pltpu.make_async_remote_copy(
            src_ref=vec.at[step, c, rows_at, :],
            dst_ref=inc.at[step, c, rows_at, :],
            send_sem=a_send.at[c, k],
            recv_sem=a_recv.at[step, c, k],
            device_id=(targets[k], grp),
            device_id_type=MESH,
        )

    def exchange(step, c):
        for k in (2, 3, 0, 1):
            @pl.when(there[k])
            def _():
                if step > 0:
                    swap(step - 1, c, k).wait_send()
                swap(step, c, k).start()

    def arrive(step, c):
        for k in (0, 1, 2, 3):
            @pl.when(there[k])
            def _():
                arrival(step, c, k).wait_recv()

    def assembled(step, c):
        return jnp.concatenate(
            [vec[step, c, :shared, :] + inc[step, c], vec[step, c, shared:, :]], axis=0
        )

    def near_copy(it, c, which):
        at = pl.ds(which * share, share)
        return pltpu.make_async_remote_copy(
            src_ref=proj.at[it, c, at, :],
            dst_ref=near.at[it, c, at, :],
            send_sem=n_send.at[c, which],
            recv_sem=n_recv.at[it, c, which],
            device_id=(sub, near_b if which else near_a),
            device_id_type=MESH,
        )

    def far_copy(it, c, which):
        at = pl.ds(which * share, share)
        return pltpu.make_async_remote_copy(
            src_ref=far_out.at[it, c, at, :],
            dst_ref=far_in.at[it, c, at, :],
            send_sem=f_send.at[c, which],
            recv_sem=f_recv.at[it, c, which],
            device_id=(sub, near_a if which else near_b),
            device_id_type=MESH,
        )

    quarter = modes // 2

    def extra_copy(which):
        return pltpu.make_async_remote_copy(
            src_ref=extra_out.at[which],
            dst_ref=extra.at[pl.ds(which * quarter, quarter), :],
            send_sem=e_send.at[which],
            recv_sem=e_recv.at[which],
            device_id=(sub, near_b if which else near_a),
            device_id_type=MESH,
        )

    eye_i = lax.broadcasted_iota(jnp.int32, (width, width), 0)
    eye_j = lax.broadcasted_iota(jnp.int32, (width, width), 1)
    lane = lax.broadcasted_iota(jnp.int32, (width, rows), 1).astype(F32)
    taken = jnp.zeros((1, rows), F32)
    for k in range(4):
        along = rows_ref[k : k + 1, :].astype(F32)
        column = jnp.sum(jnp.where(eye_i == eye_j, along, 0.0), axis=1, keepdims=True)
        hot = jnp.where(column == lane, 1.0, 0.0)
        taken = taken + jnp.sum(hot, axis=0, keepdims=True)
        hot = hot.astype(BF16)
        pick[k * piece : (k + 1) * piece, :] = hot[:piece]
        pick[middle + k * piece : middle + (k + 1) * piece, :] = hot[piece:]

    loads_in[0].wait()

    def pack_pair(top, bottom, step, j, at):
        left = left_lanes(top.shape)
        vec[step, 2 * j, at, :] = jnp.where(left, top, turn(bottom))
        vec[step, 2 * j + 1, at, :] = jnp.where(left, turn(top), bottom)

    def start(j, carry):
        at = pl.ds(pl.multiple_of(j * COLS, COLS), COLS)
        chosen = jnp.concatenate([pick[:shared, :], pick[middle : middle + shared, :]], axis=0)
        moved = select_rows(chosen, load_v[:, at])
        pack_pair(moved[:shared], moved[shared:], 0, j, pl.ds(0, shared))
        return carry

    def send_first(c, carry):
        exchange(0, c)
        return carry

    lax.fori_loop(0, blocks, start, 0)
    pl.semaphore_wait(barrier, greeted)
    lax.fori_loop(0, chunks, send_first, 0)
    loads_in[1].wait()
    extra_out[0] = cluster_v[pl.ds(pl.multiple_of((3 - near_a) * modes, modes), quarter), :]
    near_b_near_a = near_b + 1 - 2 * lax.rem(near_b, 2)
    turned = jnp.transpose(
        cluster_v[pl.ds(pl.multiple_of(near_b_near_a * modes, modes), modes), :]
    )
    extra_out[1] = turned[quarter:]
    extra_copy(0).start()
    extra_copy(1).start()

    spare = middle - shared
    free = 1.0 - taken
    order_i = lax.broadcasted_iota(jnp.int32, (rows, rows), 0)
    order_j = lax.broadcasted_iota(jnp.int32, (rows, rows), 1)
    below = jnp.where(order_i < order_j, 1.0, 0.0).astype(BF16)
    rank = dot(jnp.broadcast_to(free, (16, rows)).astype(BF16), below)[:1, :]
    place = lax.broadcasted_iota(jnp.int32, (2 * spare, rows), 0).astype(F32)
    others = jnp.where((rank == place) & (free > 0.5), 1.0, 0.0).astype(BF16)
    pick[shared:middle, :] = others[:spare]
    pick[middle + shared :, :] = others[spare:]
    for j in range(blocks):
        moved = select_rows(others, load_v[:, j * COLS : (j + 1) * COLS])
        pack_pair(moved[:spare], moved[spare:], 0, j, pl.ds(shared, spare))

    def weights(index):
        within = lax.rem(index, middle)
        total = jnp.ones(index.shape, F32)
        for k in range(4):
            inside = (within >= k * piece) & (within < (k + 1) * piece)
            total = jnp.where(inside & there[k], 0.5, total)
        return total

    row_weight = weights(lax.broadcasted_iota(jnp.int32, (rows, 1), 0))
    col_weight = weights(lax.broadcasted_iota(jnp.int32, (1, rows), 1))

    loads_in[2].wait()
    basis = row_weight * select_rows(pick[...], modes_v[...])
    high, low = split(basis)
    modes_hl[:, :modes] = high
    modes_hl[:, modes:] = low
    high, low = split(jnp.transpose(basis))
    modes_thl[:, :rows] = high
    modes_thl[:, rows:] = low

    def reorder(matrix, into, scale):
        tile = 128
        for p, part in enumerate(split(matrix[...])):
            for i in range(rows // tile):
                at = slice(i * tile, (i + 1) * tile)
                moved = dot(pick[at, :], part).astype(BF16)
                moved = dot(moved, pick_t[...])
                if scale is not None:
                    moved = moved * (scale * row_weight[at, :] * col_weight)
                into[at, p * rows : (p + 1) * rows] = moved.astype(BF16)

    def project(it, c):
        step = 2 * it
        arrive(step, c)
        sides = parts(assembled(step, c))
        rhs[c] = sides
        terms = jnp.transpose(dot(modes_thl[...], twice(sides)))
        if it > 0:
            for which in range(2):
                near_copy(it - 1, c, which).wait_send()
        proj[it, c] = terms[:HALF] + terms[HALF:]
        near_copy(it, c, 0).start()
        near_copy(it, c, 1).start()

    def fine(it, j):
        step = 2 * it + 1
        sides = jnp.concatenate([rhs[2 * j], rhs[2 * j + 1]], axis=1)
        both = dot(solve_hl[...], twice(sides))
        vec[step, 2 * j] = fold(both[:, :COLS])
        vec[step, 2 * j + 1] = fold(both[:, COLS:])

    def pairs():
        def block(k):
            return 0.5 * cluster_v[pl.ds(pl.multiple_of(k * modes, modes), modes), :]

        to_a, to_b, same = block(near_a), block(near_b), block(grp)
        extra_copy(0).wait_recv()
        extra_copy(1).wait_recv()
        cross = 0.5 * extra[...]
        first = jnp.concatenate(
            [
                jnp.concatenate([jnp.transpose(to_b), same], axis=1),
                jnp.concatenate([jnp.transpose(cross), to_a], axis=1),
            ],
            axis=0,
        )
        second = jnp.concatenate(
            [
                jnp.concatenate([jnp.transpose(to_a), same], axis=1),
                jnp.concatenate([cross, to_b], axis=1),
            ],
            axis=0,
        )
        pair_h[0], pair_l[0] = split(first)
        pair_h[1], pair_l[1] = split(second)

    def combine(it, c):
        for which in range(2):
            at = slice(which * share, (which + 1) * share)
            near_copy(it, c, which).wait_recv()
            known = jnp.concatenate([proj[it, c, at, :], near[it, c, at, :]], axis=1)
            high, low = split(known)
            mixed = dot(jnp.concatenate([high, low], axis=0), pair_h[which])
            mixed = mixed[:share] + mixed[share:] + dot(high, pair_l[which])
            if it > 0:
                far_copy(it - 1, c, which).wait_send()
            far_out[it, c, at, :] = mixed[:, :modes]
            far_copy(it, c, which).start()
            own[c, at, :] = mixed[:, modes:]

    def correct(it, c):
        for which in range(2):
            far_copy(it, c, which).wait_recv()
        coarse = own[c] + far_in[it, c]
        high = coarse.astype(BF16).astype(F32)
        sides = jnp.transpose(jnp.concatenate([high, coarse - high], axis=0)).astype(BF16)
        step = 2 * it + 1
        vec[step, c] = vec[step, c] + fold(dot(modes_hl[...], twice(sides)))
        exchange(step, c)

    def advance(it, c):
        step = 2 * it + 1
        arrive(step, c)
        value = assembled(step, c)
        if it > 0:
            value = value + xs[c]
        xs[c] = value
        vec[step + 1, c] = vec[0, c] - fold(dot(schur_hl[...], twice(parts(value))))
        exchange(step + 1, c)

    def every(stage, it, count):
        def body(c, carry):
            stage(it, c)
            return carry

        lax.fori_loop(0, count, body, 0)

    for it in range(ITERS):
        every(project, it, chunks)
        if it == 0:
            for tile in range(rows // 128):
                at = slice(tile * 128, (tile + 1) * 128)
                pick_t[:, at] = jnp.transpose(pick[at, :].astype(F32)).astype(BF16)
            pairs()
            loads_in[3].wait()
            reorder(solve_v, solve_hl, 0.5)
        if it > 0:
            every(fine, it, blocks)
        every(combine, it, chunks)
        if it == 0:
            every(fine, it, blocks)
            loads_in[4].wait()
            reorder(schur_v, schur_hl, None)
        every(correct, it, chunks)
        every(advance, it, chunks)

    def unpacked(first, second):
        left = left_lanes(first.shape)
        return jnp.concatenate(
            [jnp.where(left, first, turn(second)), jnp.where(left, turn(first), second)], axis=0
        )

    for j in range(blocks):
        at = slice(j * COLS, (j + 1) * COLS)
        out_x[:, at] = 0.5 * select_rows(pick_t[...], unpacked(xs[2 * j], xs[2 * j + 1]))
    write_x = pltpu.make_async_copy(out_x, both_out.at[0], out_sem.at[0])
    write_x.start()
    last = 2 * ITERS
    writes = []
    for j in range(blocks):
        at = slice(j * COLS, (j + 1) * COLS)
        arrive(last, 2 * j)
        arrive(last, 2 * j + 1)
        value = unpacked(assembled(last, 2 * j), assembled(last, 2 * j + 1))
        out_r[j] = 0.5 * select_rows(pick_t[...], value)
        write = pltpu.make_async_copy(
            out_r.at[j], both_out.at[1, :, pl.ds(j * COLS, COLS)], out_sem.at[1 + j]
        )
        write.start()
        writes.append(write)

    extra_copy(0).wait_send()
    extra_copy(1).wait_send()

    def drain(c, carry):
        for k in range(4):
            @pl.when(there[k])
            def _():
                swap(last, c, k).wait_send()
        for which in range(2):
            near_copy(ITERS - 1, c, which).wait_send()
            far_copy(ITERS - 1, c, which).wait_send()
        return carry

    lax.fori_loop(0, chunks, drain, 0)
    write_x.wait()
    for write in writes:
        write.wait()


def local(load_terms, schur_matrix, local_inverse, coarse_modes, cluster_inverse, row_blocks):
    rows, loads = load_terms.shape[2:]
    modes = coarse_modes.shape[3]
    width = row_blocks.shape[3]
    blocks = loads // COLS
    chunks = 2 * blocks
    steps = 2 * ITERS + 1
    any_spec = pl.BlockSpec(memory_space=pl.ANY)
    vmem_spec = pl.BlockSpec(memory_space=pltpu.VMEM)
    dma = pltpu.SemaphoreType.DMA
    halves = pl.pallas_call(
        kernel,
        out_shape=jax.ShapeDtypeStruct((2, rows, loads), F32),
        in_specs=[any_spec] * 5 + [vmem_spec],
        out_specs=any_spec,
        scratch_shapes=[
            pltpu.VMEM((rows, loads), F32),
            pltpu.VMEM((rows, rows), F32),
            pltpu.VMEM((rows, rows), F32),
            pltpu.VMEM((rows, modes), F32),
            pltpu.VMEM(cluster_inverse.shape[1:], F32),
            pltpu.VMEM((rows, rows), BF16),
            pltpu.VMEM((rows, rows), BF16),
            pltpu.VMEM((rows, 2 * rows), BF16),
            pltpu.VMEM((rows, 2 * rows), BF16),
            pltpu.VMEM((rows, 2 * modes), BF16),
            pltpu.VMEM((modes, 2 * rows), BF16),
            pltpu.VMEM((2, 2 * modes, 2 * modes), BF16),
            pltpu.VMEM((2, 2 * modes, 2 * modes), BF16),
            pltpu.VMEM((modes, modes), F32),
            pltpu.VMEM((2, modes // 2, modes), F32),
            pltpu.VMEM((steps, chunks, rows // 2, COLS), F32),
            pltpu.VMEM((steps, chunks, 2 * width, COLS), F32),
            pltpu.VMEM((chunks, rows // 2, COLS), F32),
            pltpu.VMEM((chunks, rows, COLS), BF16),
            pltpu.VMEM((ITERS, chunks, HALF, modes), F32),
            pltpu.VMEM((ITERS, chunks, HALF, modes), F32),
            pltpu.VMEM((chunks, HALF, modes), F32),
            pltpu.VMEM((ITERS, chunks, HALF, modes), F32),
            pltpu.VMEM((ITERS, chunks, HALF, modes), F32),
            pltpu.VMEM((rows, loads), F32),
            pltpu.VMEM((blocks, rows, COLS), F32),
            dma((5,)),
            dma((1 + blocks,)),
            dma((chunks, 4)),
            dma((steps, chunks, 4)),
            dma((chunks, 2)),
            dma((ITERS, chunks, 2)),
            dma((chunks, 2)),
            dma((ITERS, chunks, 2)),
            dma((2,)),
            dma((2,)),
        ],
        compiler_params=pltpu.CompilerParams(
            collective_id=0, has_side_effects=True, vmem_limit_bytes=60 * 1024 * 1024
        ),
    )(
        load_terms[0, 0], schur_matrix[0, 0], local_inverse[0, 0], coarse_modes[0, 0],
        cluster_inverse[0], row_blocks[0, 0],
    )
    return 2.0 * halves[0][None, None], 2.0 * halves[1][None, None]


def solution(mesh):
    return jax.shard_map(
        local,
        mesh=mesh,
        in_specs=(
            P("sub", "grp", None, None),
            P("sub", "grp", None, None),
            P("sub", "grp", None, None),
            P("sub", "grp", None, None),
            P("sub", None, "grp"),
            P("sub", "grp", None, None),
        ),
        out_specs=(P("sub", "grp", None, None), P("sub", "grp", None, None)),
        check_vma=False,
    )
```
